128 devices in a mesh: corpus: 4 (over x), blk: 32 (over z, y, core).
Axes of the slice: x: 4, y: 4, z: 4, core: 2. Of those that a mesh axis runs over, the one named last changes fastest.
Arguments:
- embedding: bfloat16 [32768, 1024], P(('corpus', 'blk'))
- cluster: int32 [32768], P(('corpus', 'blk')), may hold values from 0 to 7, as said below
- order: int32 [32768], P(('corpus', 'blk')), may hold values from 0 to 32767, each once
Outputs:
- nearest: float32 [32768], P(('corpus', 'blk'))
The draws below stay inside these ranges and needn't reach their ends.
Inputs may be any that keep to these rules, and one draw needn't show every extreme that they name: On every device, at most 128 documents have clusters with any one value of cluster mod 4. All devices with the same blk index have one common value that exactly 128 of their documents take. `order`: each number appears once.
All inputs are finite; a program needn't handle non-finite values.
Results may differ from the reference program's by a relative error of at most 0.0013.
Values may be sent and summed in bfloat16 or wider, within the bound.
No kernel may reach another device: no remote copies, remote signals or barrier semaphores. Data moves between devices by JAX's collectives and lax.ppermute only.
A program may use at most 128 MiB of HBM per device.

```python
import jax
import jax.numpy as jnp
from jax import lax

E = 1024
DOC_DEV = 256
CLUS_OWN = 2
DOCS = 32768
N_CORPUS = 4
N_BLK = 32


def cluster_table(key):
    devices = N_CORPUS * N_BLK
    base = jax.random.fold_in(key, 4242)
    heavy = jax.random.randint(jax.random.fold_in(base, 1), (N_BLK,), 0, N_CORPUS)
    scores = jax.random.randint(jax.random.fold_in(base, 2), (devices, DOC_DEV), 0, 1 << 16)
    scores = scores * DOC_DEV + jnp.arange(DOC_DEV, dtype=jnp.int32)[None, :]
    ranks = jnp.argsort(jnp.argsort(scores, axis=1), axis=1)
    heavy_dev = jnp.tile(heavy, N_CORPUS)[:, None]
    offset = jax.random.randint(jax.random.fold_in(base, 3), (devices, DOC_DEV), 1, N_CORPUS)
    device_offset = jax.random.randint(jax.random.fold_in(base, 6), (devices, 1), 1, N_CORPUS)
    whole_flag = jax.random.randint(jax.random.fold_in(base, 7), (devices, 1), 0, 2) == 1
    forced = jax.random.randint(jax.random.fold_in(base, 8), (), 0, devices)
    whole_flag = whole_flag | (jnp.arange(devices, dtype=jnp.int32)[:, None] == forced)
    offset = jnp.where(whole_flag, device_offset, offset)
    target = jnp.where(ranks < DOC_DEV // 2, heavy_dev, (heavy_dev + offset) % N_CORPUS)
    first = jax.random.randint(jax.random.fold_in(base, 4), (devices, DOC_DEV), 0, CLUS_OWN)
    second = jax.random.randint(jax.random.fold_in(base, 5), (devices, DOC_DEV), 0, CLUS_OWN)
    return (jnp.minimum(first, second) * N_CORPUS + target).reshape(-1).astype(jnp.int32)


def draw_cluster(key, part):
    return cluster_table(key)


def draw_embedding(key, part):
    labels = cluster_table(key)
    base = jax.random.normal(jax.random.fold_in(key, 91), (DOCS, E), jnp.float32)
    noise = jax.random.normal(jax.random.fold_in(key, 92), (DOCS, E), jnp.float32)
    flags = jax.random.randint(jax.random.fold_in(key, 93), (DOCS,), 0, 2)
    sorted_idx = jnp.argsort(labels, stable=True)
    keys_sorted = labels[sorted_idx]
    prev_idx = jnp.concatenate([sorted_idx[:1], sorted_idx[:-1]])
    same = jnp.concatenate([jnp.zeros((1,), dtype=bool), keys_sorted[1:] == keys_sorted[:-1]])
    copied = same & (flags[sorted_idx] == 1)
    mixed = jnp.where(copied[:, None], 0.6 * base[prev_idx] + 0.8 * noise[sorted_idx], base[sorted_idx])
    positions = jnp.arange(DOCS, dtype=jnp.int32)
    back_step = jax.random.randint(jax.random.fold_in(key, 95), (DOCS,), DOC_DEV, 4 * DOC_DEV)
    source = positions - back_step
    source_safe = jnp.maximum(source, 0)
    far_same = (source >= 0) & (keys_sorted[source_safe] == keys_sorted)
    dup_pick = jax.random.randint(jax.random.fold_in(key, 96), (DOCS,), 0, 5) == 0
    take = far_same & dup_pick
    extra = jax.random.normal(jax.random.fold_in(key, 97), (DOCS, E), jnp.float32)
    mixed = jnp.where(take[:, None], 0.98 * mixed[source_safe] + 0.2 * extra, mixed)
    result = jnp.zeros_like(base).at[sorted_idx].set(mixed)
    return result.astype(jnp.bfloat16)


def setup_inputs(seed: int = 0) -> dict:
    arg_keys = jax.random.split(jax.random.key(seed), 4)
    return {
        "embedding": draw_embedding(jax.random.fold_in(arg_keys[3], 71), 0),
        "cluster": draw_cluster(jax.random.fold_in(arg_keys[3], 71), 0),
        "order": jax.random.permutation(arg_keys[2], DOCS).astype(jnp.int32),
    }


def reference(embedding, cluster, order):
    wide = embedding.astype(jnp.float32)
    unit = (wide * lax.rsqrt(lax.optimization_barrier(jnp.sum(wide * wide, axis=1, keepdims=True)) + 1e-06)).astype(jnp.bfloat16)
    total = unit.shape[0]
    block = min(512, total)

    def one_block(start):
        rows = lax.dynamic_slice_in_dim(unit, start, block, 0)
        keys = lax.dynamic_slice_in_dim(cluster, start, block, 0)
        ranks = lax.dynamic_slice_in_dim(order, start, block, 0)
        sims = lax.dot_general(rows, unit, (((1,), (1,)), ((), ())), preferred_element_type=jnp.float32)
        keep = (keys[:, None] == cluster[None, :]) & (order[None, :] < ranks[:, None])
        return lax.optimization_barrier(jnp.max(jnp.where(keep, sims, jnp.float32(-1.0)), axis=1))
    starts = (jnp.arange(total // block, dtype=jnp.int32) * block).astype(jnp.int32)
    return lax.map(one_block, starts).reshape(-1)
```

```python
import functools

import jax
import jax.numpy as jnp
from jax import lax
from jax.experimental import pallas as pl
from jax.experimental.pallas import tpu as pltpu
from jax.sharding import PartitionSpec as P

AXES = ("corpus", "blk")
ROWS = 256
TAIL = 16
CLUSTER_STEP = 32768.0


def pair(v):
    return v ^ 1


def cross(v):
    return ((((v - 1) % 4) ^ 1) + 1) % 4


def exchange(name):
    move = {"X": (0, pair), "Z": (1, pair), "Y": (2, pair), "C": (3, pair)}
    move |= {"x": (0, cross), "z": (1, cross), "y": (2, cross)}
    axis, fn = move[name]
    perm = []
    for x in range(4):
        for z in range(4):
            for y in range(4):
                for c in range(2):
                    there = [x, z, y, c]
                    there[axis] = fn(there[axis])
                    a, b, d, e = there
                    perm.append((x * 32 + z * 8 + y * 2 + c, a * 32 + b * 8 + d * 2 + e))
    return perm


PERMS = {name: exchange(name) for name in "XZYCxzy"}


def swap(value, name):
    return lax.ppermute(value, AXES, PERMS[name])


def prepare_kernel(emb_ref, cluster_ref, order_ref, out_ref):
    wide = emb_ref[...].astype(jnp.float32)
    scale = lax.rsqrt(jnp.sum(wide * wide, axis=1, keepdims=True) + 1e-06)
    out_ref[pl.ds(0, ROWS), :] = (wide * scale).astype(jnp.bfloat16)
    order = order_ref[...]
    parts = [cluster_ref[...], order >> 7, order & 127, jnp.zeros_like(order)]
    keys = jnp.concatenate([p.astype(jnp.float32) for p in parts], axis=1)
    out_ref[pl.ds(ROWS, TAIL), :] = jnp.broadcast_to(keys, (TAIL, 4 * ROWS)).astype(jnp.bfloat16)


def prepare(embedding, cluster, order):
    return pl.pallas_call(
        prepare_kernel,
        out_shape=jax.ShapeDtypeStruct((ROWS + TAIL, embedding.shape[1]), jnp.bfloat16),
        in_specs=[pl.BlockSpec(memory_space=pltpu.VMEM)] * 3,
        out_specs=pl.BlockSpec(memory_space=pltpu.VMEM),
    )(embedding, cluster.reshape(1, -1), order.reshape(1, -1))


def key_of(tail):
    row = tail[pl.ds(0, TAIL), :].astype(jnp.float32)[:1]
    return row[:, :ROWS] * CLUSTER_STEP + row[:, ROWS : 2 * ROWS] * 128.0 + row[:, 2 * ROWS : 3 * ROWS]


def nearest_kernel(layout, *refs):
    row_layout, col_layout = layout
    n_row, n_col = len(row_layout), len(col_layout)
    n_in = sum(len(b) for b in row_layout) + sum(len(b) for b in col_layout)
    ins, (out_ref, held_r, tail_r, held_c, tail_c, best, key_r, base_r, key_c, sems) = (
        refs[:n_in],
        refs[n_in:],
    )
    copies = []
    at = 0
    count = 0
    for blocks, held, tail in ((row_layout, held_r, tail_r), (col_layout, held_c, tail_c)):
        for b, pieces in enumerate(blocks):
            mine = []
            start = 0
            for size in pieces:
                ref = ins[at]
                at += 1
                body = min(size, ROWS - start)
                mine.append(
                    pltpu.make_async_copy(
                        ref.at[pl.ds(0, body)], held.at[pl.ds(b * ROWS + start, body)], sems.at[count]
                    )
                )
                count += 1
                start += body
                if size > body:
                    mine.append(
                        pltpu.make_async_copy(
                            ref.at[pl.ds(body, TAIL)], tail.at[pl.ds(b * TAIL, TAIL)], sems.at[count]
                        )
                    )
                    count += 1
            copies.append(mine)
    for mine in copies:
        for copy in mine:
            copy.start()
    best[...] = jnp.full_like(best, -1.0)
    for b in range(n_row):
        for copy in copies[b]:
            copy.wait()
        keys = key_of(tail_r.at[pl.ds(b * TAIL, TAIL)])
        tall = jnp.broadcast_to(keys, (128, ROWS)).T
        key_r[pl.ds(b * ROWS, ROWS), :] = tall
        base_r[pl.ds(b * ROWS, ROWS), :] = jnp.floor(tall * (1.0 / CLUSTER_STEP)) * CLUSTER_STEP
    for b in range(n_col):
        for copy in copies[n_row + b]:
            copy.wait()
        key_c[pl.ds(b, 1), :] = key_of(tail_c.at[pl.ds(b * TAIL, TAIL)])

    def step(j, carry):
        sims = lax.dot_general(
            held_r[...],
            held_c[pl.ds(pl.multiple_of(j * ROWS, ROWS), ROWS), :],
            (((1,), (1,)), ((), ())),
            preferred_element_type=jnp.float32,
        )
        theirs = key_c[pl.ds(j, 1), :]
        top = best[...]
        for q in range(ROWS // 128):
            lanes = slice(q * 128, (q + 1) * 128)
            keep = (theirs[:, lanes] < key_r[...]) & (theirs[:, lanes] >= base_r[...])
            top = jnp.maximum(top, jnp.where(keep, sims[:, lanes], -1.0))
        best[...] = top
        return carry

    lax.fori_loop(0, n_col, step, 0)
    for b in range(n_row):
        out_ref[pl.ds(b, 1), :] = jnp.max(best[pl.ds(b * ROWS, ROWS), :].T, axis=0, keepdims=True)


def nearest(rows, cols):
    layout = tuple(tuple(tuple(p.shape[0] for p in b) for b in side) for side in (rows, cols))
    n_row, n_col = len(rows), len(cols)
    flat = [p for side in (rows, cols) for b in side for p in b]
    n_copy = sum(len(b) + 1 for side in (rows, cols) for b in side)
    width = flat[0].shape[1]
    return pl.pallas_call(
        functools.partial(nearest_kernel, layout),
        out_shape=jax.ShapeDtypeStruct((n_row, ROWS), jnp.float32),
        in_specs=[pl.BlockSpec(memory_space=pl.ANY)] * len(flat),
        out_specs=pl.BlockSpec(memory_space=pltpu.VMEM),
        scratch_shapes=[
            pltpu.VMEM((n_row * ROWS, width), jnp.bfloat16),
            pltpu.VMEM((n_row * TAIL, width), jnp.bfloat16),
            pltpu.VMEM((n_col * ROWS, width), jnp.bfloat16),
            pltpu.VMEM((n_col * TAIL, width), jnp.bfloat16),
            pltpu.VMEM((n_row * ROWS, 128), jnp.float32),
            pltpu.VMEM((n_row * ROWS, 128), jnp.float32),
            pltpu.VMEM((n_row * ROWS, 128), jnp.float32),
            pltpu.VMEM((n_col, ROWS), jnp.float32),
            pltpu.SemaphoreType.DMA((n_copy,)),
        ],
        compiler_params=pltpu.CompilerParams(vmem_limit_bytes=48 << 20),
        cost_estimate=pl.CostEstimate(
            flops=2 * n_row * n_col * ROWS * ROWS * width,
            bytes_accessed=(n_row + n_col) * ROWS * width * 2,
            transcendentals=0,
        ),
    )(*flat)


def cube(own, names):
    a, b, c = names
    got = {"": (own,)}
    for k in names:
        got[k] = (swap(own, k),)
    got[a + b] = (swap(got[b][0], a),)
    got[b + c] = (swap(got[c][0], b),)
    got[a + c] = (swap(got[a][0], c),)
    half = ROWS // 2
    got[a + b + c] = (swap(got[b + c][0][:half], a), swap(got[a + b][0][half:], c))
    return got


def local(embedding, cluster, order):
    own = prepare(embedding, cluster, order)
    b_names, a_names = "xzy", "XZY"
    b = cube(own, b_names)
    a = cube(own, a_names)
    both = {k: (v, tuple(swap(p, "C") for p in v)) for k, v in b.items()}
    near_a = ["", "X", "Z", "Y"]
    near_b = [v for k in ("", "x", "z", "y") for v in both[k]]
    mid_b = [v for k in ("xz", "zy", "xy") for v in both[k]]
    far_a = ["XZ", "ZY", "XY", "XZY"]
    far_b = list(both["xzy"])
    r1 = nearest([a[k] for k in near_a], near_b)
    r2 = nearest([a[k] for k in near_a], mid_b)
    r3 = nearest([a[k] for k in far_a], near_b + mid_b)
    r4 = nearest([a[k] for k in near_a + far_a], far_b)
    names = near_a + far_a
    best = jnp.maximum(r4, jnp.concatenate([jnp.maximum(r1, r2), r3], axis=0))
    slot = {k: best[i : i + 1] for i, k in enumerate(names)}
    x = swap(jnp.concatenate([slot[k] for k in ("X", "XZ", "XY", "XZY")], axis=0), "X")
    kept = jnp.maximum(x, jnp.concatenate([slot[k] for k in ("", "Z", "Y", "ZY")], axis=0))
    z = swap(jnp.concatenate([kept[1:2], kept[3:4]], axis=0), "Z")
    kept = jnp.maximum(z, jnp.concatenate([kept[0:1], kept[2:3]], axis=0))
    return jnp.maximum(swap(kept[1], "Y"), kept[0])


def solution(mesh):
    in_specs = (P(AXES, None), P(AXES), P(AXES))
    return jax.shard_map(local, mesh=mesh, in_specs=in_specs, out_specs=P(AXES), check_vma=False)
```

```python
import functools

import jax
import jax.numpy as jnp
from jax import lax
from jax.experimental import pallas as pl
from jax.experimental.pallas import tpu as pltpu
from jax.sharding import PartitionSpec as P


AXES = ("corpus", "blk")
ROWS = 256
TAIL = 16
BLOCK = ROWS + TAIL
VMEM_LIMIT = 32 << 20
CLUSTER_STEP = 32768.0


def pair(v):
    return v ^ 1


def cross(v):
    return ((((v - 1) % 4) ^ 1) + 1) % 4


def exchange(name):
    move = {"X": (0, pair), "Z": (1, pair), "Y": (2, pair), "C": (3, pair)}
    move |= {"x": (0, cross), "z": (1, cross), "y": (2, cross)}
    axis, fn = move[name]
    perm = []
    for x in range(4):
        for z in range(4):
            for y in range(4):
                for c in range(2):
                    there = [x, z, y, c]
                    there[axis] = fn(there[axis])
                    a, b, d, e = there
                    perm.append((x * 32 + z * 8 + y * 2 + c, a * 32 + b * 8 + d * 2 + e))
    return perm


PERMS = {name: exchange(name) for name in "XZYCxzy"}


def swap(value, name):
    return lax.ppermute(value, AXES, PERMS[name])


def prepare_kernel(emb_ref, cluster_ref, order_ref, out_ref):
    wide = emb_ref[...].astype(jnp.float32)
    scale = lax.rsqrt(jnp.sum(wide * wide, axis=1, keepdims=True) + 1e-06)
    out_ref[pl.ds(0, ROWS), :] = (wide * scale).astype(jnp.bfloat16)
    order = order_ref[...]
    parts = [cluster_ref[...], order >> 7, order & 127, jnp.zeros_like(order)]
    keys = jnp.concatenate([p.astype(jnp.float32) for p in parts], axis=1)
    out_ref[pl.ds(ROWS, TAIL), :] = jnp.broadcast_to(keys, (TAIL, 4 * ROWS)).astype(jnp.bfloat16)


def prepare(embedding, cluster, order):
    return pl.pallas_call(
        prepare_kernel,
        out_shape=jax.ShapeDtypeStruct((ROWS + TAIL, embedding.shape[1]), jnp.bfloat16),
        in_specs=[pl.BlockSpec(memory_space=pltpu.VMEM)] * 3,
        out_specs=pl.BlockSpec(memory_space=pltpu.VMEM),
    )(embedding, cluster.reshape(1, -1), order.reshape(1, -1))


def pile_keys(pile, i):
    row = pile[pl.ds(i * BLOCK + ROWS, TAIL), :].astype(jnp.float32)[:1]
    return row[:, :ROWS] * CLUSTER_STEP + row[:, ROWS : 2 * ROWS] * 128.0 + row[:, 2 * ROWS : 3 * ROWS]


def nearest_kernel(n_row, n_col, loops, *refs):
    n = len(n_row) + len(n_col)
    rows, cols = refs[: len(n_row)], refs[len(n_row) : n]
    out_ref, best, key_r, base_r, key_c = refs[n:]
    first_row = [sum(n_row[:i]) for i in range(len(n_row))]
    first_col = [sum(n_col[:i]) for i in range(len(n_col))]
    best[...] = jnp.full_like(best, -1.0)
    for p, pile in enumerate(rows):
        for i in range(n_row[p]):
            at = (first_row[p] + i) * BLOCK
            tall = jnp.broadcast_to(pile_keys(pile, i), (128, ROWS)).T
            key_r[pl.ds(at, ROWS), :] = tall
            base_r[pl.ds(at, ROWS), :] = jnp.floor(tall * (1.0 / CLUSTER_STEP)) * CLUSTER_STEP
            key_r[pl.ds(at + ROWS, TAIL), :] = jnp.full((TAIL, 128), -1.0, jnp.float32)
            base_r[pl.ds(at + ROWS, TAIL), :] = jnp.zeros((TAIL, 128), jnp.float32)
    for p, pile in enumerate(cols):
        for i in range(n_col[p]):
            key_c[pl.ds(first_col[p] + i, 1), :] = pile_keys(pile, i)
    for p, c in loops:
        mine = pl.ds(first_row[p] * BLOCK, n_row[p] * BLOCK)

        def tile(j, p=p, c=c, mine=mine):
            start = j * BLOCK if isinstance(j, int) else pl.multiple_of(j * BLOCK, TAIL)
            sims = lax.dot_general(
                rows[p][...],
                cols[c][pl.ds(start, ROWS), :],
                (((1,), (1,)), ((), ())),
                preferred_element_type=jnp.float32,
            )
            theirs = key_c[pl.ds(first_col[c] + j, 1), :]
            top = best[mine, :]
            for q in range(ROWS // 128):
                lanes = slice(q * 128, (q + 1) * 128)
                keep = (theirs[:, lanes] < key_r[mine, :]) & (theirs[:, lanes] >= base_r[mine, :])
                top = jnp.maximum(top, jnp.where(keep, sims[:, lanes], -1.0))
            best[mine, :] = top

        if n_row[p] == 1:
            for j in range(n_col[c]):
                tile(j)
        else:
            lax.fori_loop(0, n_col[c], lambda j, carry, tile=tile: (tile(j), carry)[1], 0)
    for b in range(sum(n_row)):
        out_ref[pl.ds(b, 1), :] = jnp.max(best[pl.ds(b * BLOCK, ROWS), :].T, axis=0, keepdims=True)


def nearest(rows, cols, loops=None):
    n_row = tuple(v.shape[0] // BLOCK for v in rows)
    n_col = tuple(v.shape[0] // BLOCK for v in cols)
    loops = loops or tuple((r, c) for r in range(len(rows)) for c in range(len(cols)))
    width = rows[0].shape[1]
    tall = sum(n_row) * BLOCK
    return pl.pallas_call(
        functools.partial(nearest_kernel, n_row, n_col, loops),
        out_shape=jax.ShapeDtypeStruct((sum(n_row), ROWS), jnp.float32),
        in_specs=[pl.BlockSpec(memory_space=pltpu.VMEM)] * (len(rows) + len(cols)),
        out_specs=pl.BlockSpec(memory_space=pltpu.VMEM),
        scratch_shapes=[
            pltpu.VMEM((tall, 128), jnp.float32),
            pltpu.VMEM((tall, 128), jnp.float32),
            pltpu.VMEM((tall, 128), jnp.float32),
            pltpu.VMEM((sum(n_col), ROWS), jnp.float32),
        ],
        compiler_params=pltpu.CompilerParams(vmem_limit_bytes=VMEM_LIMIT),
        cost_estimate=pl.CostEstimate(
            flops=2 * sum(n_row[r] * n_col[c] for r, c in loops) * ROWS * ROWS * width,
            bytes_accessed=(sum(n_row) + sum(n_col)) * ROWS * width * 2,
            transcendentals=0,
        ),
    )(*rows, *cols)


def near(own, names):
    return {"": own} | {k: swap(own, k) for k in names}


def mid(got, names):
    pairs = [(names[i], names[(i + 1) % 3]) for i in range(3)]
    return [swap(got[k], link) for link, k in pairs]


def stacked(*blocks):
    return jnp.concatenate(blocks, axis=0)


def steps(embedding, cluster, order):
    own = prepare(embedding, cluster, order)
    b_names, a_names = "xzy", "XZY"
    b = near(own, b_names)
    a = near(own, a_names)
    b_mid = mid(b, b_names)
    a_mid = mid(a, a_names)
    near_a = stacked(*(a[k] for k in ("", *a_names)))
    other = swap(stacked(*(b[k] for k in b_names)), "C")
    near_b = stacked(*(b[k] for k in ("", *b_names)), swap(own, "C"))
    r1 = nearest([near_a], [near_b])
    b_mid, r1 = lax.optimization_barrier((b_mid, r1))
    b_far = swap(b_mid[1], "x")
    mid_b = stacked(*b_mid)
    mid_other = swap(mid_b, "C")
    r2 = nearest([near_a], [other, mid_b])
    a_mid, mid_other, r2 = lax.optimization_barrier((a_mid, mid_other, r2))
    a_far = swap(a_mid[1], "X")
    mid_a = stacked(*a_mid)
    both_a = stacked(near_a, mid_a)
    r3a = nearest([both_a], [mid_other])
    r3b = nearest([mid_a], [near_b, other, mid_b])
    b_far, a_far, r3a, r3b = lax.optimization_barrier((b_far, a_far, r3a, r3b))
    far_b = stacked(b_far, swap(b_far, "C"))
    r4a = nearest([a_far], [near_b, other, mid_b, mid_other])
    r4b = nearest([stacked(both_a, a_far)], [far_b])
    r3 = jnp.concatenate([jnp.maximum(jnp.maximum(r1, r2), r3a[:4]), jnp.maximum(r3b, r3a[4:]), r4a], axis=0)
    best = jnp.maximum(r3, r4b)
    names = ["", *a_names, "XZ", "ZY", "XY", "XZY"]
    slot = {k: best[i : i + 1] for i, k in enumerate(names)}
    x = swap(jnp.concatenate([slot[k] for k in ("X", "XZ", "XY", "XZY")], axis=0), "X")
    kept = jnp.maximum(x, jnp.concatenate([slot[k] for k in ("", "Z", "Y", "ZY")], axis=0))
    z = swap(jnp.concatenate([kept[1:2], kept[3:4]], axis=0), "Z")
    kept = jnp.maximum(z, jnp.concatenate([kept[0:1], kept[2:3]], axis=0))
    return jnp.maximum(swap(kept[1], "Y"), kept[0])


def solution(mesh):
    in_specs = (P(AXES, None), P(AXES), P(AXES))
    return jax.shard_map(steps, mesh=mesh, in_specs=in_specs, out_specs=P(AXES), check_vma=False)
```
